32 devices in a mesh: vec: 4 (over y, x), orb: 8 (over z, core).
Axes of the slice: x: 2, y: 2, z: 4, core: 2. Of those that a mesh axis runs over, the one named last changes fastest.
Arguments:
- chol_occ: float32 [44, 96, 1056], P('vec', 'orb'), may hold values from -6 to 6
- chol_vir: float32 [44, 960, 1056], P('vec', 'orb'), may hold values from -6 to 6
- singles: float32 [96, 960], P('orb'), may hold values from -0.6 to 0.6
Outputs:
- dressed_vir: float32 [44, 960, 1056], P('vec', 'orb')
- dressed_ov: float32 [44, 96, 960], P(None, 'orb', 'vec')
- fock_ov: float32 [96, 960], P('orb')
The draws below stay inside these ranges and needn't reach their ends.
All inputs are finite; a program needn't handle non-finite values.
Results may differ from the reference program's by a relative error of at most 0.000086.
Values sent between devices are 32-bit elements; how exact they have to be, the bound alone decides.
A program may use at most 64 MiB of HBM per device.

```python
import jax
import jax.numpy as jnp
from jax import lax

O = 96
V = 960
N = 1056
Q = 44


def block_scale(key, shape, shards, smallest, largest):
    level, own = 1.0, jax.random.fold_in(key, 6)
    for position, shards_of in shards:
        steps = jnp.exp(jax.random.uniform(jax.random.fold_in(own, position), (shards_of,), jnp.float32, smallest / len(shards), largest / len(shards)))
        level = level * jnp.repeat(steps, shape[position] // shards_of).reshape([-1 if axis == position else 1 for axis in range(len(shape))])
    return level


def bell_draw(own_key, extent, scale, most, cuts=(), kind=jnp.bfloat16):
    result = scale * jax.random.normal(own_key, extent, jnp.float32)
    if cuts:
        result = result * block_scale(own_key, extent, cuts, -0.22, 0.18)
    return jnp.clip(result, -most, most).astype(kind)


def setup_inputs(seed: int = 0) -> dict:
    key_list = jax.random.split(jax.random.key(seed), 4)
    return {
        "chol_occ": bell_draw(key_list[0], (Q, O, N), 1.0, 6.0, ((0, 4), (1, 8)), jnp.float32),
        "chol_vir": bell_draw(key_list[1], (Q, V, N), 1.0, 6.0, ((0, 4), (1, 8)), jnp.float32),
        "singles": bell_draw(key_list[2], (O, V), 0.1, 0.6, ((0, 8),), jnp.float32),
    }


def dress_right(matrix_rows, singles):
    occ_cols = matrix_rows[:, :, :O]
    extra_term = jnp.einsum("qrj,ja->qra", occ_cols, singles, precision=lax.Precision.HIGHEST)
    return jnp.concatenate([occ_cols, matrix_rows[:, :, O:] + extra_term], axis=2)


def reference(chol_occ, chol_vir, singles):
    singles_t = singles.T

    def one_vector(pair_input):
        occ_vector, vir_vector = pair_input
        left_rows = vir_vector - jnp.dot(singles_t, occ_vector, precision=lax.Precision.HIGHEST)
        return dress_right(left_rows[None], singles)[0]

    dressed_vir = lax.map(one_vector, (chol_occ, chol_vir))
    dressed_occ = dress_right(chol_occ, singles)
    dressed_ov = dressed_occ[:, :, O:]
    traces = jnp.trace(chol_occ[:, :, :O], axis1=1, axis2=2)
    fock_ov = jnp.einsum("q,qia->ia", traces, dressed_ov, precision=lax.Precision.HIGHEST) / Q
    return dressed_vir, dressed_ov, fock_ov
```

```python
import jax
import jax.numpy as jnp
from jax import lax
from jax.experimental import pallas as pl
from jax.experimental.pallas import tpu as pltpu
from jax.sharding import PartitionSpec as P

MESH = pl.DeviceIdType.MESH
F32, BF16 = jnp.float32, jnp.bfloat16
LANES = 128
CORES = 2
SKEW = 1
AHEAD = 4
FIRST = 5
RATE = 2


def split(x):
    hi = x.astype(BF16)
    return hi, (x - hi.astype(F32)).astype(BF16)


def dot(a, b):
    return jnp.dot(a, b, preferred_element_type=F32)


def make_kernel(W, D, Q, R, RV, N, A):
    OCC = N - A
    NZ = D // CORES
    GR = 8 if R % 8 == 0 else (4 if R % 4 == 0 else R)
    NJ = R // GR
    ROWS = Q * R
    GRAN = Q * NJ
    MAIN = N // LANES * LANES
    TAIL = N - MAIN
    SLOTS = LANES // TAIL if TAIL else 1
    GROUPS = -(-Q // SLOTS)
    PIECE = A // W
    KP = -(-OCC // LANES) * LANES
    UNITS = Q + 1
    NP = -(-N // LANES) * LANES
    AP = -(-A // LANES) * LANES
    VP = -(-RV // LANES) * LANES
    TILES = AP // LANES
    CH = -(-TILES // W)
    NCH = -(-TILES // CH)
    HT = GROUPS * NJ
    HS = HT + 1
    HEAD = HS + NJ * CH
    LAG = SKEW * max(NZ - 2, 0)
    STEPS = UNITS + LAG
    START = max(FIRST, LAG + 1)

    def kernel(occ, vir, sing, out_vir, out_ov, out_fock,
               gath, head, amps, vloc, oloc, sloc, xbuf, drows, tmat, tright, sleft, lwts,
               ovsend, ovrecv, ovout, fbuf, fout,
               s_right, s_left, s_part, r_dir, r_part, a_s, a_r, ov_s, ov_r, f_s, f_r,
               in_sem, v_in, v_out, o_out):
        v = lax.axis_index("vec")
        o = lax.axis_index("orb")
        z = o // CORES
        k = o % CORES
        has_r = z < NZ - 1
        has_l = z > 0
        right = lax.rem(o + CORES, D)
        left = lax.rem(o - CORES + D, D)
        part = z * CORES + (1 - k)

        c_occ = pltpu.make_async_copy(occ, oloc, in_sem.at[0])
        c_sing = pltpu.make_async_copy(sing, sloc, in_sem.at[1])
        c_occ.start()
        c_sing.start()

        c_vir = pltpu.make_async_copy(vir, vloc, v_in.at[0])

        def vout(q):
            return pltpu.make_async_copy(vloc.at[q], out_vir.at[q], v_out.at[0])

        bar = pltpu.get_barrier_semaphore()

        @pl.when(has_r)
        def _():
            pl.semaphore_signal(bar, inc=1, device_id=(v, right), device_id_type=MESH)

        @pl.when(has_l)
        def _():
            pl.semaphore_signal(bar, inc=1, device_id=(v, left), device_id_type=MESH)

        pl.semaphore_signal(bar, inc=1, device_id=(v, part), device_id_type=MESH)
        for h in range(1, W):
            pl.semaphore_signal(bar, inc=1, device_id=(lax.rem(v + h, W), o), device_id_type=MESH)

        def piece(c, s, u):
            if isinstance(u, str):
                return head.at[c, s], 0, 0
            return gath.at[c, s, pl.ds(u * NJ, NJ)], u + 1, 1

        def remote(s, u, sems, target):
            ref, i, kind = piece(k, s, u)
            return pltpu.make_async_remote_copy(
                src_ref=ref, dst_ref=ref, send_sem=sems.at[s, kind], recv_sem=r_dir.at[s, i],
                device_id=(v, target), device_id_type=MESH)

        def across(s, u):
            ref, i, kind = piece(k, s, u)
            return pltpu.make_async_remote_copy(
                src_ref=ref, dst_ref=ref, send_sem=s_part.at[s, kind], recv_sem=r_part.at[i],
                device_id=(v, part), device_id_type=MESH)

        def send_own(u):
            @pl.when(has_r)
            def _():
                remote(z, u, s_right, right).start()

            @pl.when(has_l)
            def _():
                remote(z, u, s_left, left).start()

            across(z, u).start()

        def relay(h, u):
            @pl.when(z - h >= 0)
            def _():
                s = z - h
                remote(s, u, s_right, right).wait_recv()

                @pl.when(has_r)
                def _():
                    remote(s, u, s_right, right).start()

                across(s, u).start()

            @pl.when(z + h < NZ)
            def _():
                s = z + h
                remote(s, u, s_left, left).wait_recv()

                @pl.when(has_l)
                def _():
                    remote(s, u, s_left, left).start()

                across(s, u).start()

        def from_partner(u):
            if isinstance(u, str):
                ref, i = head.at[1 - k], 0
            else:
                ref, i = gath.at[1 - k, :, pl.ds(u * NJ, NJ)], u + 1
            pltpu.make_async_remote_copy(
                src_ref=ref, dst_ref=ref, send_sem=s_part.at[0, 0], recv_sem=r_part.at[i],
                device_id=(v, part), device_id_type=MESH).wait_recv()

        def finish():
            for s in range(NZ):
                for kind, ref in enumerate((head.at[k, s], gath.at[k, s])):
                    def drain(sems, target):
                        pltpu.make_async_remote_copy(
                            src_ref=ref, dst_ref=ref, send_sem=sems.at[s, kind], recv_sem=r_dir.at[s, 0],
                            device_id=(v, target), device_id_type=MESH).wait_send()

                    @pl.when(jnp.logical_and(s <= z, has_r))
                    def _():
                        drain(s_right, right)

                    @pl.when(jnp.logical_and(s >= z, has_l))
                    def _():
                        drain(s_left, left)

                    drain(s_part, part)

        def a_copy(h):
            w = lax.rem(v + h, W)
            c = lax.rem(v, NCH)
            return pltpu.make_async_remote_copy(
                src_ref=head.at[:, :, pl.ds(HS, NJ * CH)], dst_ref=amps.at[c], send_sem=a_s.at[h],
                recv_sem=a_r.at[c], device_id=(w, o), device_id_type=MESH)

        def a_wait(c):
            @pl.when(c != v)
            def _():
                pltpu.make_async_remote_copy(
                    src_ref=amps.at[c], dst_ref=amps.at[c], send_sem=a_s.at[0],
                    recv_sem=a_r.at[c], device_id=(lax.rem(v + 1, W), o), device_id_type=MESH).wait_recv()

        def repack(q):
            for j in range(NJ):
                gath[k, z, q * NJ + j] = oloc[q, j * GR:(j + 1) * GR, 0:MAIN]

        units = ["h"] + list(range(Q))
        c_occ.wait()
        c_sing.wait()
        full = sloc[...]
        if NCH * CH * LANES > A:
            full = jnp.concatenate([full, jnp.zeros((R, NCH * CH * LANES - A), F32)], axis=1)
        mine = lax.rem(v, NCH)
        for t in range(CH):
            val = full[:, t * LANES:(t + 1) * LANES]
            for c in range(1, NCH):
                at = (c * CH + t) * LANES
                val = jnp.where(mine == c, full[:, at:at + LANES], val)
            for j in range(NJ):
                head[k, z, HS + j * CH + t] = val[j * GR:(j + 1) * GR]
        if TAIL:
            for g in range(GROUPS):
                parts = [oloc[min(g * SLOTS + t, Q - 1), :, MAIN:N] for t in range(SLOTS)]
                packed = jnp.concatenate(parts, axis=1) if SLOTS > 1 else parts[0]
                for j in range(NJ):
                    head[k, z, g * NJ + j, :, 0:SLOTS * TAIL] = packed[j * GR:(j + 1) * GR]
        ri = lax.broadcasted_iota(jnp.int32, (R, KP), 0) + o * R
        ci = lax.broadcasted_iota(jnp.int32, (R, KP), 1)
        mask = ri == ci
        lane = lax.broadcasted_iota(jnp.int32, (GR, LANES), 1)
        tr = jnp.zeros((GR, LANES), F32)
        for q in range(Q):
            dq = jnp.sum(jnp.where(mask, oloc[q, :, 0:KP], 0.0), axis=0, keepdims=True)
            tq = jnp.sum(dq, axis=1, keepdims=True)
            tr = tr + jnp.where(lane == q, jnp.broadcast_to(tq, (GR, LANES)), 0.0)
        head[k, z, HT] = tr
        for q in range(Q):
            repack(q)

        pl.semaphore_wait(bar, has_r.astype(jnp.int32) + has_l.astype(jnp.int32) + W)

        for u in units[:AHEAD]:
            send_own(u)
        c_vir.start()

        for q in range(Q):
            for r in range(R):
                drows[r * Q + q:r * Q + q + 1, :] = oloc[q, r:r + 1, :]

        for t in range(START):
            if AHEAD <= t + AHEAD < UNITS:
                send_own(units[t + AHEAD])
            for h in range(1, NZ):
                n = t - SKEW * (h - 1)
                if 0 <= n < UNITS:
                    relay(h, units[n])
            if t == LAG:
                from_partner("h")

                @pl.when(v < NCH)
                def _():
                    for h in range(1, W):
                        a_copy(h).start()

        for c in range(NCH):
            a_wait(c)

            @pl.when(c == v)
            def _():
                amps[c] = head[:, :, HS:HS + NJ * CH]

        xbuf[...] = jnp.zeros_like(xbuf)
        for d in range(D):
            for j in range(NJ):
                at = d * R + j * GR
                for t in range(TILES):
                    xbuf[at:at + GR, t * LANES:(t + 1) * LANES] = (
                        amps[t // CH, d % CORES, d // CORES, j * CH + t % CH])
        amp = xbuf[0:OCC, 0:A]
        tmat[...] = jnp.zeros_like(tmat)
        shifted = jnp.concatenate([jnp.zeros((OCC, OCC), F32), amp], axis=1)
        thi, tlo = split(shifted)
        tmat[0:OCC, :] = thi
        tmat[KP:KP + OCC, :] = tlo
        thi, tlo = split(jnp.transpose(xbuf[:, 0:AP])[0:A])
        tright[:, 0:KP] = thi
        tright[:, KP:2 * KP] = tlo
        ahi, alo = split(xbuf[:, 0:A])
        pick = (lax.broadcasted_iota(jnp.int32, (A, VP), 0)
                == lax.broadcasted_iota(jnp.int32, (A, VP), 1) + o * RV)
        pick = jnp.where(pick, 1.0, 0.0).astype(BF16)
        shi = dot(ahi, pick).astype(BF16)
        sleft[0:KP, 0:VP] = shi
        sleft[KP:2 * KP, 0:VP] = shi
        sleft[0:KP, VP:2 * VP] = dot(alo, pick).astype(BF16)
        sleft[KP:2 * KP, VP:2 * VP] = jnp.zeros((KP, VP), BF16)
        lwts[...] = jnp.zeros_like(lwts)

        keep = lax.broadcasted_iota(jnp.int32, (ROWS, KP), 1) < OCC
        hi, lo = split(jnp.where(keep, drows[:, 0:KP], 0.0))
        extra = dot(jnp.concatenate([hi, hi], axis=1), tmat[...]) + dot(lo, tmat[0:KP, :])
        drows[...] = drows[...] + extra
        for w in range(W):
            sl = drows[:, OCC + w * PIECE:OCC + (w + 1) * PIECE]
            for r in range(R):
                ovsend[w, r] = sl[r * Q:(r + 1) * Q]
        total = head[0, 0, HT]
        for d in range(1, D):
            total = total + head[d % CORES, d // CORES, HT]
        rid = lax.broadcasted_iota(jnp.int32, (R, ROWS), 0) * Q
        cid = lax.broadcasted_iota(jnp.int32, (R, ROWS), 1)
        wts = jnp.zeros((R, ROWS), F32)
        for q in range(Q):
            wts = wts + jnp.where(cid == rid + q, jnp.broadcast_to(total[0:1, q:q + 1], (R, ROWS)), 0.0)
        whi, wlo = split(wts)
        dhi, dlo = split(drows[...])
        fock = (dot(whi, dhi) + (dot(whi, dlo) + dot(wlo, dhi)))[:, OCC:]
        for j in range(NJ):
            fbuf[v, j] = fock[j * GR:(j + 1) * GR]

        def ov_copy(h):
            w = lax.rem(v + h, W)
            return pltpu.make_async_remote_copy(
                src_ref=ovsend.at[w], dst_ref=ovrecv.at[v], send_sem=ov_s.at[h],
                recv_sem=ov_r.at[h], device_id=(w, o), device_id_type=MESH)

        def f_copy(h):
            w = lax.rem(v + h, W)
            return pltpu.make_async_remote_copy(
                src_ref=fbuf.at[v], dst_ref=fbuf.at[v], send_sem=f_s.at[h],
                recv_sem=f_r.at[h], device_id=(w, o), device_id_type=MESH)

        for h in range(1, W):
            ov_copy(h).start()
            f_copy(h).start()
        ovrecv[v] = ovsend[v]

        c_vir.wait()

        def dress(q):
            from_partner(q)
            if TAIL:
                shift = lax.rem(LANES - lax.rem(q, SLOTS) * TAIL, LANES)
            for d in range(D):
                for j in range(NJ):
                    at = d * R + j * GR
                    xbuf[at:at + GR, 0:MAIN] = gath[d % CORES, d // CORES, q * NJ + j]
                    if TAIL:
                        t = pltpu.roll(head[d % CORES, d // CORES, (q // SLOTS) * NJ + j], shift, axis=1)
                        xbuf[at:at + GR, MAIN:N] = t[:, 0:TAIL]
            hi, lo = split(jnp.transpose(xbuf[...])[0:N])
            prod = dot(jnp.concatenate([hi, lo], axis=1), sleft[...])
            prod = prod[:, 0:VP] + prod[:, VP:2 * VP]
            vloc[q] = vloc[q] - prod[:, 0:RV]
            hi, lo = split(vloc[q, 0:OCC, :])
            lwts[0:OCC, 0:RV] = hi
            lwts[KP:KP + OCC, 0:RV] = hi
            lwts[0:OCC, VP:VP + RV] = lo
            prod = dot(tright[...], lwts[...])
            prod = prod[:, 0:VP] + prod[:, VP:2 * VP]
            vloc[q, OCC:N, :] = vloc[q, OCC:N, :] + prod[:, 0:RV]
            vout(q).start()

        def done(t):
            return jnp.minimum(t - LAG, RATE * (t - START + 1))

        @pl.loop(START, STEPS)
        def _(t):
            @pl.when(t + AHEAD < UNITS)
            def _():
                send_own(t + AHEAD - 1)

            for h in range(1, NZ):
                n = t - SKEW * (h - 1)

                @pl.when(n < UNITS)
                def _():
                    relay(h, n - 1)

            lo = jnp.where(t == START, 0, done(t - 1))

            @pl.loop(lo, done(t))
            def _(q):
                dress(q)

        for h in range(1, W):
            ov_copy(h).wait_recv()
            f_copy(h).wait_recv()
        for w in range(W):
            for r in range(R):
                ovout[r, w * Q:(w + 1) * Q, :] = ovrecv[w, r]
        c_ov = pltpu.make_async_copy(ovout, out_ov, o_out.at[0])
        c_ov.start()
        for j in range(NJ):
            acc = fbuf[0, j]
            for w in range(1, W):
                acc = acc + fbuf[w, j]
            fout[j * GR:(j + 1) * GR, :] = acc / (Q * W)
        c_f = pltpu.make_async_copy(fout, out_fock, o_out.at[1])
        c_f.start()

        finish()
        pltpu.make_async_copy(vloc, out_vir, v_out.at[0]).wait()

        @pl.when(v < NCH)
        def _():
            for h in range(1, W):
                a_copy(h).wait_send()

        for h in range(1, W):
            ov_copy(h).wait_send()
            f_copy(h).wait_send()
        c_ov.wait()
        c_f.wait()

    DMA = pltpu.SemaphoreType.DMA
    V = pltpu.VMEM
    any_spec = pl.BlockSpec(memory_space=pl.ANY)
    return pl.pallas_call(
        kernel,
        name="dress",
        out_shape=(jax.ShapeDtypeStruct((Q, N, RV), F32),
                   jax.ShapeDtypeStruct((R, Q * W, PIECE), F32),
                   jax.ShapeDtypeStruct((R, A), F32)),
        in_specs=[pl.BlockSpec(memory_space=pltpu.HBM)] * 3,
        out_specs=(any_spec,) * 3,
        scratch_shapes=[
            V((CORES, NZ, GRAN, GR, MAIN), F32),
            V((CORES, NZ, HEAD, GR, LANES), F32),
            V((NCH, CORES, NZ, NJ * CH, GR, LANES), F32),
            V((Q, N, RV), F32),
            V((Q, R, N), F32),
            V((R, A), F32),
            V((KP, NP), F32),
            V((ROWS, N), F32),
            V((2 * KP, N), BF16),
            V((A, 2 * KP), BF16),
            V((2 * KP, 2 * VP), BF16),
            V((2 * KP, 2 * VP), BF16),
            V((W, R, Q, PIECE), F32),
            V((W, R, Q, PIECE), F32),
            V((R, Q * W, PIECE), F32),
            V((W, NJ, GR, A), F32),
            V((R, A), F32),
            DMA((NZ, 2)), DMA((NZ, 2)), DMA((NZ, 2)), DMA((NZ, UNITS)), DMA((UNITS,)),
            DMA((W,)), DMA((NCH,)), DMA((W,)), DMA((W,)), DMA((W,)), DMA((W,)),
            DMA((2,)), DMA((1,)), DMA((1,)), DMA((2,)),
        ],
        compiler_params=pltpu.CompilerParams(
            collective_id=0, has_side_effects=True, vmem_limit_bytes=40 * 2**20),
    )


def write_out(*refs):
    n = (len(refs) - 1) // 2
    copies = [pltpu.make_async_copy(refs[i], refs[n + i], refs[-1].at[i]) for i in range(n)]
    for c in copies:
        c.start()
    for c in copies:
        c.wait()


def store(arrays):
    return pl.pallas_call(
        write_out,
        name="store",
        out_shape=tuple(jax.ShapeDtypeStruct(a.shape, a.dtype) for a in arrays),
        in_specs=[pl.BlockSpec(memory_space=pl.ANY)] * len(arrays),
        out_specs=(pl.BlockSpec(memory_space=pltpu.HBM),) * len(arrays),
        scratch_shapes=[pltpu.SemaphoreType.DMA((len(arrays),))],
        compiler_params=pltpu.CompilerParams(vmem_limit_bytes=2**20),
    )(*arrays)


def solution(mesh):
    W, D = mesh.shape["vec"], mesh.shape["orb"]

    def shards(chol_occ, chol_vir, singles):
        Q, R, N = chol_occ.shape
        call = make_kernel(W, D, Q, R, chol_vir.shape[1], N, singles.shape[1])
        args = (chol_occ, jnp.swapaxes(chol_vir, 1, 2), singles)
        vir, ov, fock = store(call(*(pltpu.with_memory_space_constraint(a, pltpu.HBM) for a in args)))
        return jnp.swapaxes(vir, 1, 2), jnp.swapaxes(ov, 0, 1), fock

    return jax.shard_map(
        shards,
        mesh=mesh,
        in_specs=(P("vec", "orb", None), P("vec", "orb", None), P("orb", None)),
        out_specs=(P("vec", "orb", None), P(None, "orb", "vec"), P("orb", None)),
        check_vma=False,
    )
```

```python
import jax
import jax.numpy as jnp
from jax import lax
from jax.experimental import pallas as pl
from jax.experimental.pallas import tpu as pltpu
from jax.sharding import PartitionSpec as P

MESH = pl.DeviceIdType.MESH
F32, BF16 = jnp.float32, jnp.bfloat16
LANES = 128
CORES = 2
SKEW = 1
AHEAD = 8
FIRST = 5
RATE = 2


def split(x):
    hi = x.astype(BF16)
    return hi, (x - hi.astype(F32)).astype(BF16)


def dot(a, b):
    return jnp.dot(a, b, preferred_element_type=F32)


def make_kernel(W, D, Q, R, RV, N, A):
    OCC = N - A
    NZ = D // CORES
    GR = 8 if R % 8 == 0 else (4 if R % 4 == 0 else R)
    NJ = R // GR
    ROWS = Q * R
    GRAN = Q * NJ
    MAIN = N // LANES * LANES
    TAIL = N - MAIN
    SLOTS = LANES // TAIL if TAIL else 1
    GROUPS = -(-Q // SLOTS)
    PIECE = A // W
    KP = -(-OCC // LANES) * LANES
    UNITS = Q + 1
    NP = -(-N // LANES) * LANES
    AP = -(-A // LANES) * LANES
    VP = -(-RV // LANES) * LANES
    TILES = AP // LANES
    CH = -(-TILES // W)
    NCH = -(-TILES // CH)
    HT = GROUPS * NJ
    HS = HT + 1
    HEAD = HS + NJ * CH
    LAG = SKEW * max(NZ - 2, 0)
    STEPS = UNITS + LAG
    START = max(FIRST, LAG + 1)

    def kernel(occ, vir, sing, out_vir, out_ov, out_fock,
               gath, head, amps, vloc, oloc, sloc, xbuf, drows, tmat, tright, sleft, lwts,
               ovsend, ovrecv, ovout, fbuf, fout,
               s_right, s_left, s_part, r_dir, r_part, a_s, a_r, ov_s, ov_r, f_s, f_r,
               in_sem, v_in, v_out, o_out):
        v = lax.axis_index("vec")
        o = lax.axis_index("orb")
        z = o // CORES
        k = o % CORES
        has_r = z < NZ - 1
        has_l = z > 0
        right = lax.rem(o + CORES, D)
        left = lax.rem(o - CORES + D, D)
        part = z * CORES + (1 - k)

        c_occ = pltpu.make_async_copy(occ, oloc, in_sem.at[0])
        c_sing = pltpu.make_async_copy(sing, sloc, in_sem.at[1])
        c_occ.start()
        c_sing.start()

        c_vir = pltpu.make_async_copy(vir, vloc, v_in.at[0])

        def vout(q):
            return pltpu.make_async_copy(vloc.at[q], out_vir.at[q], v_out.at[0])

        bar = pltpu.get_barrier_semaphore()

        @pl.when(has_r)
        def _():
            pl.semaphore_signal(bar, inc=1, device_id=(v, right), device_id_type=MESH)

        @pl.when(has_l)
        def _():
            pl.semaphore_signal(bar, inc=1, device_id=(v, left), device_id_type=MESH)

        pl.semaphore_signal(bar, inc=1, device_id=(v, part), device_id_type=MESH)
        for h in range(1, W):
            pl.semaphore_signal(bar, inc=1, device_id=(lax.rem(v + h, W), o), device_id_type=MESH)

        def piece(c, s, u):
            if isinstance(u, str):
                return head.at[c, s], 0, 0
            return gath.at[c, s, pl.ds(u * NJ, NJ)], u + 1, 1

        def remote(s, u, sems, target):
            ref, i, kind = piece(k, s, u)
            return pltpu.make_async_remote_copy(
                src_ref=ref, dst_ref=ref, send_sem=sems.at[s, kind], recv_sem=r_dir.at[s, i],
                device_id=(v, target), device_id_type=MESH)

        def across(s, u):
            ref, i, kind = piece(k, s, u)
            return pltpu.make_async_remote_copy(
                src_ref=ref, dst_ref=ref, send_sem=s_part.at[s, kind], recv_sem=r_part.at[i],
                device_id=(v, part), device_id_type=MESH)

        def send_own(u):
            @pl.when(has_r)
            def _():
                remote(z, u, s_right, right).start()

            @pl.when(has_l)
            def _():
                remote(z, u, s_left, left).start()

            across(z, u).start()

        def relay(h, u):
            @pl.when(z - h >= 0)
            def _():
                s = z - h
                remote(s, u, s_right, right).wait_recv()

                @pl.when(has_r)
                def _():
                    remote(s, u, s_right, right).start()

                across(s, u).start()

            @pl.when(z + h < NZ)
            def _():
                s = z + h
                remote(s, u, s_left, left).wait_recv()

                @pl.when(has_l)
                def _():
                    remote(s, u, s_left, left).start()

                across(s, u).start()

        def from_partner(u):
            if isinstance(u, str):
                ref, i = head.at[1 - k], 0
            else:
                ref, i = gath.at[1 - k, :, pl.ds(u * NJ, NJ)], u + 1
            pltpu.make_async_remote_copy(
                src_ref=ref, dst_ref=ref, send_sem=s_part.at[0, 0], recv_sem=r_part.at[i],
                device_id=(v, part), device_id_type=MESH).wait_recv()

        def finish():
            for s in range(NZ):
                for kind, ref in enumerate((head.at[k, s], gath.at[k, s])):
                    def drain(sems, target):
                        pltpu.make_async_remote_copy(
                            src_ref=ref, dst_ref=ref, send_sem=sems.at[s, kind], recv_sem=r_dir.at[s, 0],
                            device_id=(v, target), device_id_type=MESH).wait_send()

                    @pl.when(jnp.logical_and(s <= z, has_r))
                    def _():
                        drain(s_right, right)

                    @pl.when(jnp.logical_and(s >= z, has_l))
                    def _():
                        drain(s_left, left)

                    drain(s_part, part)

        def a_copy(h):
            w = lax.rem(v + h, W)
            c = lax.rem(v, NCH)
            return pltpu.make_async_remote_copy(
                src_ref=head.at[:, :, pl.ds(HS, NJ * CH)], dst_ref=amps.at[c], send_sem=a_s.at[h],
                recv_sem=a_r.at[c], device_id=(w, o), device_id_type=MESH)

        def a_wait(c):
            @pl.when(c != v)
            def _():
                pltpu.make_async_remote_copy(
                    src_ref=amps.at[c], dst_ref=amps.at[c], send_sem=a_s.at[0],
                    recv_sem=a_r.at[c], device_id=(lax.rem(v + 1, W), o), device_id_type=MESH).wait_recv()

        def repack(q):
            for j in range(NJ):
                gath[k, z, q * NJ + j] = oloc[q, j * GR:(j + 1) * GR, 0:MAIN]

        units = ["h"] + list(range(Q))
        c_occ.wait()
        c_sing.wait()
        full = sloc[...]
        if NCH * CH * LANES > A:
            full = jnp.concatenate([full, jnp.zeros((R, NCH * CH * LANES - A), F32)], axis=1)
        mine = lax.rem(v, NCH)
        for t in range(CH):
            val = full[:, t * LANES:(t + 1) * LANES]
            for c in range(1, NCH):
                at = (c * CH + t) * LANES
                val = jnp.where(mine == c, full[:, at:at + LANES], val)
            for j in range(NJ):
                head[k, z, HS + j * CH + t] = val[j * GR:(j + 1) * GR]
        if TAIL:
            for g in range(GROUPS):
                parts = [oloc[min(g * SLOTS + t, Q - 1), :, MAIN:N] for t in range(SLOTS)]
                packed = jnp.concatenate(parts, axis=1) if SLOTS > 1 else parts[0]
                for j in range(NJ):
                    head[k, z, g * NJ + j, :, 0:SLOTS * TAIL] = packed[j * GR:(j + 1) * GR]
        ri = lax.broadcasted_iota(jnp.int32, (R, KP), 0) + o * R
        ci = lax.broadcasted_iota(jnp.int32, (R, KP), 1)
        mask = ri == ci
        lane = lax.broadcasted_iota(jnp.int32, (GR, LANES), 1)
        tr = jnp.zeros((GR, LANES), F32)
        for q in range(Q):
            dq = jnp.sum(jnp.where(mask, oloc[q, :, 0:KP], 0.0), axis=0, keepdims=True)
            tq = jnp.sum(dq, axis=1, keepdims=True)
            tr = tr + jnp.where(lane == q, jnp.broadcast_to(tq, (GR, LANES)), 0.0)
        head[k, z, HT] = tr
        for q in range(Q):
            repack(q)

        pl.semaphore_wait(bar, has_r.astype(jnp.int32) + has_l.astype(jnp.int32) + W)

        for u in units[:AHEAD]:
            send_own(u)
        c_vir.start()

        for q in range(Q):
            for r in range(R):
                drows[r * Q + q:r * Q + q + 1, :] = oloc[q, r:r + 1, :]

        for t in range(START):
            if AHEAD <= t + AHEAD < UNITS:
                send_own(units[t + AHEAD])
            for h in range(1, NZ):
                n = t - SKEW * (h - 1)
                if 0 <= n < UNITS:
                    relay(h, units[n])
            if t == LAG:
                from_partner("h")

                @pl.when(v < NCH)
                def _():
                    for h in range(1, W):
                        a_copy(h).start()

        for c in range(NCH):
            a_wait(c)

            @pl.when(c == v)
            def _():
                amps[c] = head[:, :, HS:HS + NJ * CH]

        xbuf[...] = jnp.zeros_like(xbuf)
        for d in range(D):
            for j in range(NJ):
                at = d * R + j * GR
                for t in range(TILES):
                    xbuf[at:at + GR, t * LANES:(t + 1) * LANES] = (
                        amps[t // CH, d % CORES, d // CORES, j * CH + t % CH])
        amp = xbuf[0:OCC, 0:A]
        tmat[...] = jnp.zeros_like(tmat)
        shifted = jnp.concatenate([jnp.zeros((OCC, OCC), F32), amp], axis=1)
        thi, tlo = split(shifted)
        tmat[0:OCC, :] = thi
        tmat[KP:KP + OCC, :] = tlo
        thi, tlo = split(jnp.transpose(xbuf[:, 0:AP])[0:A])
        tright[:, 0:KP] = thi
        tright[:, KP:2 * KP] = tlo
        ahi, alo = split(xbuf[:, 0:A])
        pick = (lax.broadcasted_iota(jnp.int32, (A, VP), 0)
                == lax.broadcasted_iota(jnp.int32, (A, VP), 1) + o * RV)
        pick = jnp.where(pick, 1.0, 0.0).astype(BF16)
        shi = dot(ahi, pick).astype(BF16)
        sleft[0:KP, 0:VP] = shi
        sleft[KP:2 * KP, 0:VP] = shi
        sleft[0:KP, VP:2 * VP] = dot(alo, pick).astype(BF16)
        sleft[KP:2 * KP, VP:2 * VP] = jnp.zeros((KP, VP), BF16)
        lwts[...] = jnp.zeros_like(lwts)

        keep = lax.broadcasted_iota(jnp.int32, (ROWS, KP), 1) < OCC
        hi, lo = split(jnp.where(keep, drows[:, 0:KP], 0.0))
        extra = dot(jnp.concatenate([hi, hi], axis=1), tmat[...]) + dot(lo, tmat[0:KP, :])
        drows[...] = drows[...] + extra
        for w in range(W):
            sl = drows[:, OCC + w * PIECE:OCC + (w + 1) * PIECE]
            for r in range(R):
                ovsend[w, r] = sl[r * Q:(r + 1) * Q]
        total = head[0, 0, HT]
        for d in range(1, D):
            total = total + head[d % CORES, d // CORES, HT]
        rid = lax.broadcasted_iota(jnp.int32, (R, ROWS), 0) * Q
        cid = lax.broadcasted_iota(jnp.int32, (R, ROWS), 1)
        wts = jnp.zeros((R, ROWS), F32)
        for q in range(Q):
            wts = wts + jnp.where(cid == rid + q, jnp.broadcast_to(total[0:1, q:q + 1], (R, ROWS)), 0.0)
        whi, wlo = split(wts)
        dhi, dlo = split(drows[...])
        fock = (dot(whi, dhi) + (dot(whi, dlo) + dot(wlo, dhi)))[:, OCC:]
        for j in range(NJ):
            fbuf[v, j] = fock[j * GR:(j + 1) * GR]

        def ov_copy(h):
            w = lax.rem(v + h, W)
            return pltpu.make_async_remote_copy(
                src_ref=ovsend.at[w], dst_ref=ovrecv.at[v], send_sem=ov_s.at[h],
                recv_sem=ov_r.at[h], device_id=(w, o), device_id_type=MESH)

        def f_copy(h):
            w = lax.rem(v + h, W)
            return pltpu.make_async_remote_copy(
                src_ref=fbuf.at[v], dst_ref=fbuf.at[v], send_sem=f_s.at[h],
                recv_sem=f_r.at[h], device_id=(w, o), device_id_type=MESH)

        for h in range(1, W):
            ov_copy(h).start()
            f_copy(h).start()
        ovrecv[v] = ovsend[v]

        c_vir.wait()

        def dress(q):
            from_partner(q)
            if TAIL:
                shift = lax.rem(LANES - lax.rem(q, SLOTS) * TAIL, LANES)
            for d in range(D):
                for j in range(NJ):
                    at = d * R + j * GR
                    xbuf[at:at + GR, 0:MAIN] = gath[d % CORES, d // CORES, q * NJ + j]
                    if TAIL:
                        t = pltpu.roll(head[d % CORES, d // CORES, (q // SLOTS) * NJ + j], shift, axis=1)
                        xbuf[at:at + GR, MAIN:N] = t[:, 0:TAIL]
            hi, lo = split(jnp.transpose(xbuf[...])[0:N])
            prod = dot(jnp.concatenate([hi, lo], axis=1), sleft[...])
            prod = prod[:, 0:VP] + prod[:, VP:2 * VP]
            vloc[q] = vloc[q] - prod[:, 0:RV]
            hi, lo = split(vloc[q, 0:OCC, :])
            lwts[0:OCC, 0:RV] = hi
            lwts[KP:KP + OCC, 0:RV] = hi
            lwts[0:OCC, VP:VP + RV] = lo
            prod = dot(tright[...], lwts[...])
            prod = prod[:, 0:VP] + prod[:, VP:2 * VP]
            vloc[q, OCC:N, :] = vloc[q, OCC:N, :] + prod[:, 0:RV]
            vout(q).start()

        def done(t):
            return jnp.where(t == STEPS - 1, Q, jnp.minimum(t - LAG - 1, RATE * (t - START + 1)))

        @pl.loop(START, STEPS)
        def _(t):
            @pl.when(t + AHEAD < UNITS)
            def _():
                send_own(t + AHEAD - 1)

            for h in range(1, NZ):
                n = t - SKEW * (h - 1)

                @pl.when(n < UNITS)
                def _():
                    relay(h, n - 1)

            lo = jnp.where(t == START, 0, done(t - 1))

            @pl.loop(lo, done(t))
            def _(q):
                dress(q)

        for h in range(1, W):
            ov_copy(h).wait_recv()
            f_copy(h).wait_recv()
        for w in range(W):
            for r in range(R):
                ovout[r, w * Q:(w + 1) * Q, :] = ovrecv[w, r]
        c_ov = pltpu.make_async_copy(ovout, out_ov, o_out.at[0])
        c_ov.start()
        for j in range(NJ):
            acc = fbuf[0, j]
            for w in range(1, W):
                acc = acc + fbuf[w, j]
            fout[j * GR:(j + 1) * GR, :] = acc / (Q * W)
        c_f = pltpu.make_async_copy(fout, out_fock, o_out.at[1])
        c_f.start()

        finish()
        pltpu.make_async_copy(vloc, out_vir, v_out.at[0]).wait()

        @pl.when(v < NCH)
        def _():
            for h in range(1, W):
                a_copy(h).wait_send()

        for h in range(1, W):
            ov_copy(h).wait_send()
            f_copy(h).wait_send()
        c_ov.wait()
        c_f.wait()

    DMA = pltpu.SemaphoreType.DMA
    V = pltpu.VMEM
    any_spec = pl.BlockSpec(memory_space=pl.ANY)
    return pl.pallas_call(
        kernel,
        name="dress",
        out_shape=(jax.ShapeDtypeStruct((Q, N, RV), F32),
                   jax.ShapeDtypeStruct((R, Q * W, PIECE), F32),
                   jax.ShapeDtypeStruct((R, A), F32)),
        in_specs=[pl.BlockSpec(memory_space=pltpu.HBM)] * 3,
        out_specs=(any_spec,) * 3,
        scratch_shapes=[
            V((CORES, NZ, GRAN, GR, MAIN), F32),
            V((CORES, NZ, HEAD, GR, LANES), F32),
            V((NCH, CORES, NZ, NJ * CH, GR, LANES), F32),
            V((Q, N, RV), F32),
            V((Q, R, N), F32),
            V((R, A), F32),
            V((KP, NP), F32),
            V((ROWS, N), F32),
            V((2 * KP, N), BF16),
            V((A, 2 * KP), BF16),
            V((2 * KP, 2 * VP), BF16),
            V((2 * KP, 2 * VP), BF16),
            V((W, R, Q, PIECE), F32),
            V((W, R, Q, PIECE), F32),
            V((R, Q * W, PIECE), F32),
            V((W, NJ, GR, A), F32),
            V((R, A), F32),
            DMA((NZ, 2)), DMA((NZ, 2)), DMA((NZ, 2)), DMA((NZ, UNITS)), DMA((UNITS,)),
            DMA((W,)), DMA((NCH,)), DMA((W,)), DMA((W,)), DMA((W,)), DMA((W,)),
            DMA((2,)), DMA((1,)), DMA((1,)), DMA((2,)),
        ],
        compiler_params=pltpu.CompilerParams(
            collective_id=0, has_side_effects=True, vmem_limit_bytes=40 * 2**20),
    )


def write_out(*refs):
    n = (len(refs) - 1) // 2
    copies = [pltpu.make_async_copy(refs[i], refs[n + i], refs[-1].at[i]) for i in range(n)]
    for c in copies:
        c.start()
    for c in copies:
        c.wait()


def store(arrays):
    return pl.pallas_call(
        write_out,
        name="store",
        out_shape=tuple(jax.ShapeDtypeStruct(a.shape, a.dtype) for a in arrays),
        in_specs=[pl.BlockSpec(memory_space=pl.ANY)] * len(arrays),
        out_specs=(pl.BlockSpec(memory_space=pltpu.HBM),) * len(arrays),
        scratch_shapes=[pltpu.SemaphoreType.DMA((len(arrays),))],
        compiler_params=pltpu.CompilerParams(vmem_limit_bytes=2**20),
    )(*arrays)


def solution(mesh):
    W, D = mesh.shape["vec"], mesh.shape["orb"]

    def shards(chol_occ, chol_vir, singles):
        Q, R, N = chol_occ.shape
        call = make_kernel(W, D, Q, R, chol_vir.shape[1], N, singles.shape[1])
        args = (chol_occ, jnp.swapaxes(chol_vir, 1, 2), singles)
        vir, ov, fock = store(call(*(pltpu.with_memory_space_constraint(a, pltpu.HBM) for a in args)))
        return jnp.swapaxes(vir, 1, 2), jnp.swapaxes(ov, 0, 1), fock

    return jax.shard_map(
        shards,
        mesh=mesh,
        in_specs=(P("vec", "orb", None), P("vec", "orb", None), P("orb", None)),
        out_specs=(P("vec", "orb", None), P(None, "orb", "vec"), P("orb", None)),
        check_vma=False,
    )
```

```python
import jax
import jax.numpy as jnp
from jax import lax
from jax.experimental import pallas as pl
from jax.experimental.pallas import tpu as pltpu
from jax.sharding import PartitionSpec as P

MESH = pl.DeviceIdType.MESH
F32, BF16 = jnp.float32, jnp.bfloat16
LANES = 128
CORES = 2
SKEW = 1
AHEAD = 5
FIRST = 5
RATE = 2


def split(x):
    hi = x.astype(BF16)
    return hi, (x - hi.astype(F32)).astype(BF16)


def dot(a, b):
    return jnp.dot(a, b, preferred_element_type=F32)


def make_kernel(W, D, Q, R, RV, N, A):
    OCC = N - A
    NZ = D // CORES
    GR = 8 if R % 8 == 0 else (4 if R % 4 == 0 else R)
    NJ = R // GR
    ROWS = Q * R
    GRAN = Q * NJ
    MAIN = N // LANES * LANES
    TAIL = N - MAIN
    SLOTS = LANES // TAIL if TAIL else 1
    GROUPS = -(-Q // SLOTS)
    PIECE = A // W
    KP = -(-OCC // LANES) * LANES
    UNITS = Q + 1
    NP = -(-N // LANES) * LANES
    AP = -(-A // LANES) * LANES
    VP = -(-RV // LANES) * LANES
    TILES = AP // LANES
    CH = -(-TILES // W)
    NCH = -(-TILES // CH)
    HT = GROUPS * NJ
    HS = HT + 1
    HEAD = HS + NJ * CH
    LAG = SKEW * max(NZ - 2, 0)
    STEPS = UNITS + LAG
    START = max(FIRST, LAG + 1)

    def kernel(occ, vir, sing, out_vir, out_ov, out_fock,
               gath, head, amps, vloc, oloc, sloc, xbuf, drows, tmat, tright, sleft, lwts,
               ovsend, ovrecv, ovout, fbuf, fout,
               s_right, s_left, s_part, r_dir, r_part, a_s, a_r, ov_s, ov_r, f_s, f_r,
               in_sem, v_in, v_out, o_out, ready):
        v = lax.axis_index("vec")
        o = lax.axis_index("orb")
        z = o // CORES
        k = o % CORES
        has_r = z < NZ - 1
        has_l = z > 0
        right = lax.rem(o + CORES, D)
        left = lax.rem(o - CORES + D, D)
        part = z * CORES + (1 - k)

        c_occ = pltpu.make_async_copy(occ, oloc, in_sem.at[0])
        c_sing = pltpu.make_async_copy(sing, sloc, in_sem.at[1])
        c_occ.start()
        c_sing.start()

        c_vir = pltpu.make_async_copy(vir, vloc, v_in.at[0])

        def vout(q):
            return pltpu.make_async_copy(vloc.at[q], out_vir.at[q], v_out.at[0])

        bar = pltpu.get_barrier_semaphore()

        @pl.when(has_r)
        def _():
            pl.semaphore_signal(bar, inc=1, device_id=(v, right), device_id_type=MESH)

        pl.semaphore_signal(bar, inc=1, device_id=(v, part), device_id_type=MESH)
        for h in range(1, W):
            @pl.when(v + h < W)
            def _():
                pl.semaphore_signal(bar, inc=1, device_id=(lax.rem(v + h, W), o), device_id_type=MESH)

        pl.semaphore_wait(bar, has_l.astype(jnp.int32) + v + 1)

        @pl.when(has_l)
        def _():
            pl.semaphore_signal(ready.at[0], inc=1, device_id=(v, left), device_id_type=MESH)

        for h in range(1, W):
            @pl.when(v - h >= 0)
            def _():
                pl.semaphore_signal(ready.at[1], inc=1, device_id=(lax.rem(v - h + W, W), o),
                                    device_id_type=MESH)

        def piece(c, s, u):
            if isinstance(u, str):
                return head.at[c, s], 0, 0
            return gath.at[c, s, pl.ds(u * NJ, NJ)], u + 1, 1

        def remote(s, u, sems, target):
            ref, i, kind = piece(k, s, u)
            return pltpu.make_async_remote_copy(
                src_ref=ref, dst_ref=ref, send_sem=sems.at[s, kind], recv_sem=r_dir.at[s, i],
                device_id=(v, target), device_id_type=MESH)

        def across(s, u):
            ref, i, kind = piece(k, s, u)
            return pltpu.make_async_remote_copy(
                src_ref=ref, dst_ref=ref, send_sem=s_part.at[s, kind], recv_sem=r_part.at[i],
                device_id=(v, part), device_id_type=MESH)

        def send_left(u):
            @pl.when(has_l)
            def _():
                remote(z, u, s_left, left).start()

            across(z, u).start()

        def send_right(u):
            @pl.when(has_r)
            def _():
                remote(z, u, s_right, right).start()

        def send_own(u):
            send_left(u)
            send_right(u)

        def relay(h, u):
            @pl.when(z - h >= 0)
            def _():
                s = z - h
                remote(s, u, s_right, right).wait_recv()

                @pl.when(has_r)
                def _():
                    remote(s, u, s_right, right).start()

                across(s, u).start()

            @pl.when(z + h < NZ)
            def _():
                s = z + h
                remote(s, u, s_left, left).wait_recv()

                @pl.when(has_l)
                def _():
                    remote(s, u, s_left, left).start()

                across(s, u).start()

        def from_partner(u):
            if isinstance(u, str):
                ref, i = head.at[1 - k], 0
            else:
                ref, i = gath.at[1 - k, :, pl.ds(u * NJ, NJ)], u + 1
            pltpu.make_async_remote_copy(
                src_ref=ref, dst_ref=ref, send_sem=s_part.at[0, 0], recv_sem=r_part.at[i],
                device_id=(v, part), device_id_type=MESH).wait_recv()

        def finish():
            for s in range(NZ):
                for kind, ref in enumerate((head.at[k, s], gath.at[k, s])):
                    def drain(sems, target):
                        pltpu.make_async_remote_copy(
                            src_ref=ref, dst_ref=ref, send_sem=sems.at[s, kind], recv_sem=r_dir.at[s, 0],
                            device_id=(v, target), device_id_type=MESH).wait_send()

                    @pl.when(jnp.logical_and(s <= z, has_r))
                    def _():
                        drain(s_right, right)

                    @pl.when(jnp.logical_and(s >= z, has_l))
                    def _():
                        drain(s_left, left)

                    drain(s_part, part)

        def a_copy(h):
            w = lax.rem(v + h, W)
            c = lax.rem(v, NCH)
            return pltpu.make_async_remote_copy(
                src_ref=head.at[:, :, pl.ds(HS, NJ * CH)], dst_ref=amps.at[c], send_sem=a_s.at[h],
                recv_sem=a_r.at[c], device_id=(w, o), device_id_type=MESH)

        def a_wait(c):
            @pl.when(c != v)
            def _():
                pltpu.make_async_remote_copy(
                    src_ref=amps.at[c], dst_ref=amps.at[c], send_sem=a_s.at[0],
                    recv_sem=a_r.at[c], device_id=(lax.rem(v + 1, W), o), device_id_type=MESH).wait_recv()

        def repack(q):
            for j in range(NJ):
                gath[k, z, q * NJ + j] = oloc[q, j * GR:(j + 1) * GR, 0:MAIN]

        units = ["h"] + list(range(Q))
        c_occ.wait()
        repack(0)
        send_left(0)
        c_sing.wait()
        full = sloc[...]
        if NCH * CH * LANES > A:
            full = jnp.concatenate([full, jnp.zeros((R, NCH * CH * LANES - A), F32)], axis=1)
        mine = lax.rem(v, NCH)
        for t in range(CH):
            val = full[:, t * LANES:(t + 1) * LANES]
            for c in range(1, NCH):
                at = (c * CH + t) * LANES
                val = jnp.where(mine == c, full[:, at:at + LANES], val)
            for j in range(NJ):
                head[k, z, HS + j * CH + t] = val[j * GR:(j + 1) * GR]
        if TAIL:
            for g in range(GROUPS):
                parts = [oloc[min(g * SLOTS + t, Q - 1), :, MAIN:N] for t in range(SLOTS)]
                packed = jnp.concatenate(parts, axis=1) if SLOTS > 1 else parts[0]
                for j in range(NJ):
                    head[k, z, g * NJ + j, :, 0:SLOTS * TAIL] = packed[j * GR:(j + 1) * GR]
        ri = lax.broadcasted_iota(jnp.int32, (R, KP), 0) + o * R
        ci = lax.broadcasted_iota(jnp.int32, (R, KP), 1)
        mask = ri == ci
        lane = lax.broadcasted_iota(jnp.int32, (GR, LANES), 1)
        tr = jnp.zeros((GR, LANES), F32)
        for q in range(Q):
            dq = jnp.sum(jnp.where(mask, oloc[q, :, 0:KP], 0.0), axis=0, keepdims=True)
            tq = jnp.sum(dq, axis=1, keepdims=True)
            tr = tr + jnp.where(lane == q, jnp.broadcast_to(tq, (GR, LANES)), 0.0)
        head[k, z, HT] = tr
        for q in range(1, Q):
            repack(q)

        for u in units[:AHEAD]:
            if u != 0:
                send_left(u)

        @pl.when(has_r)
        def _():
            pl.semaphore_wait(ready.at[0], 1)

        for u in units[:AHEAD]:
            send_right(u)
        c_vir.start()

        for q in range(Q):
            for r in range(R):
                drows[r * Q + q:r * Q + q + 1, :] = oloc[q, r:r + 1, :]

        for t in range(START):
            if AHEAD <= t + AHEAD < UNITS:
                send_own(units[t + AHEAD])
            for h in range(1, NZ):
                n = t - SKEW * (h - 1)
                if 0 <= n < UNITS:
                    relay(h, units[n])
            if t == LAG:
                from_partner("h")

                @pl.when(v < W - 1)
                def _():
                    pl.semaphore_wait(ready.at[1], W - 1 - v)

                @pl.when(v < NCH)
                def _():
                    for h in range(1, W):
                        a_copy(h).start()

        for c in range(NCH):
            a_wait(c)

            @pl.when(c == v)
            def _():
                amps[c] = head[:, :, HS:HS + NJ * CH]

        xbuf[...] = jnp.zeros_like(xbuf)
        for d in range(D):
            for j in range(NJ):
                at = d * R + j * GR
                for t in range(TILES):
                    xbuf[at:at + GR, t * LANES:(t + 1) * LANES] = (
                        amps[t // CH, d % CORES, d // CORES, j * CH + t % CH])
        amp = xbuf[0:OCC, 0:A]
        tmat[...] = jnp.zeros_like(tmat)
        shifted = jnp.concatenate([jnp.zeros((OCC, OCC), F32), amp], axis=1)
        thi, tlo = split(shifted)
        tmat[0:OCC, :] = thi
        tmat[KP:KP + OCC, :] = tlo
        thi, tlo = split(jnp.transpose(xbuf[:, 0:AP])[0:A])
        tright[:, 0:KP] = thi
        tright[:, KP:2 * KP] = tlo
        ahi, alo = split(xbuf[:, 0:A])
        pick = (lax.broadcasted_iota(jnp.int32, (A, VP), 0)
                == lax.broadcasted_iota(jnp.int32, (A, VP), 1) + o * RV)
        pick = jnp.where(pick, 1.0, 0.0).astype(BF16)
        shi = dot(ahi, pick).astype(BF16)
        sleft[0:KP, 0:VP] = shi
        sleft[KP:2 * KP, 0:VP] = shi
        sleft[0:KP, VP:2 * VP] = dot(alo, pick).astype(BF16)
        sleft[KP:2 * KP, VP:2 * VP] = jnp.zeros((KP, VP), BF16)
        lwts[...] = jnp.zeros_like(lwts)

        keep = lax.broadcasted_iota(jnp.int32, (ROWS, KP), 1) < OCC
        hi, lo = split(jnp.where(keep, drows[:, 0:KP], 0.0))
        extra = dot(jnp.concatenate([hi, hi], axis=1), tmat[...]) + dot(lo, tmat[0:KP, :])
        drows[...] = drows[...] + extra
        for w in range(W):
            sl = drows[:, OCC + w * PIECE:OCC + (w + 1) * PIECE]
            for r in range(R):
                ovsend[w, r] = sl[r * Q:(r + 1) * Q]
        total = head[0, 0, HT]
        for d in range(1, D):
            total = total + head[d % CORES, d // CORES, HT]
        rid = lax.broadcasted_iota(jnp.int32, (R, ROWS), 0) * Q
        cid = lax.broadcasted_iota(jnp.int32, (R, ROWS), 1)
        wts = jnp.zeros((R, ROWS), F32)
        for q in range(Q):
            wts = wts + jnp.where(cid == rid + q, jnp.broadcast_to(total[0:1, q:q + 1], (R, ROWS)), 0.0)
        whi, wlo = split(wts)
        dhi, dlo = split(drows[...])
        fock = (dot(whi, dhi) + (dot(whi, dlo) + dot(wlo, dhi)))[:, OCC:]
        for j in range(NJ):
            fbuf[v, j] = fock[j * GR:(j + 1) * GR]

        def ov_copy(h):
            w = lax.rem(v + h, W)
            return pltpu.make_async_remote_copy(
                src_ref=ovsend.at[w], dst_ref=ovrecv.at[v], send_sem=ov_s.at[h],
                recv_sem=ov_r.at[h], device_id=(w, o), device_id_type=MESH)

        def f_copy(h):
            w = lax.rem(v + h, W)
            return pltpu.make_async_remote_copy(
                src_ref=fbuf.at[v], dst_ref=fbuf.at[v], send_sem=f_s.at[h],
                recv_sem=f_r.at[h], device_id=(w, o), device_id_type=MESH)

        for h in range(1, W):
            ov_copy(h).start()
            f_copy(h).start()
        ovrecv[v] = ovsend[v]

        c_vir.wait()

        def dress(q):
            from_partner(q)
            if TAIL:
                shift = lax.rem(LANES - lax.rem(q, SLOTS) * TAIL, LANES)
            for d in range(D):
                for j in range(NJ):
                    at = d * R + j * GR
                    xbuf[at:at + GR, 0:MAIN] = gath[d % CORES, d // CORES, q * NJ + j]
                    if TAIL:
                        t = pltpu.roll(head[d % CORES, d // CORES, (q // SLOTS) * NJ + j], shift, axis=1)
                        xbuf[at:at + GR, MAIN:N] = t[:, 0:TAIL]
            hi, lo = split(jnp.transpose(xbuf[...])[0:N])
            prod = dot(jnp.concatenate([hi, lo], axis=1), sleft[...])
            prod = prod[:, 0:VP] + prod[:, VP:2 * VP]
            vloc[q] = vloc[q] - prod[:, 0:RV]
            hi, lo = split(vloc[q, 0:OCC, :])
            lwts[0:OCC, 0:RV] = hi
            lwts[KP:KP + OCC, 0:RV] = hi
            lwts[0:OCC, VP:VP + RV] = lo
            prod = dot(tright[...], lwts[...])
            prod = prod[:, 0:VP] + prod[:, VP:2 * VP]
            vloc[q, OCC:N, :] = vloc[q, OCC:N, :] + prod[:, 0:RV]
            vout(q).start()

        def done(t):
            return jnp.where(t == STEPS - 1, Q, jnp.minimum(t - LAG - 1, RATE * (t - START + 1)))

        @pl.loop(START, STEPS)
        def _(t):
            @pl.when(t + AHEAD < UNITS)
            def _():
                send_own(t + AHEAD - 1)

            for h in range(1, NZ):
                n = t - SKEW * (h - 1)

                @pl.when(n < UNITS)
                def _():
                    relay(h, n - 1)

            lo = jnp.where(t == START, 0, done(t - 1))

            @pl.loop(lo, done(t))
            def _(q):
                dress(q)

        for h in range(1, W):
            ov_copy(h).wait_recv()
            f_copy(h).wait_recv()
        for w in range(W):
            for r in range(R):
                ovout[r, w * Q:(w + 1) * Q, :] = ovrecv[w, r]
        c_ov = pltpu.make_async_copy(ovout, out_ov, o_out.at[0])
        c_ov.start()
        for j in range(NJ):
            acc = fbuf[0, j]
            for w in range(1, W):
                acc = acc + fbuf[w, j]
            fout[j * GR:(j + 1) * GR, :] = acc / (Q * W)
        c_f = pltpu.make_async_copy(fout, out_fock, o_out.at[1])
        c_f.start()

        finish()
        pltpu.make_async_copy(vloc, out_vir, v_out.at[0]).wait()

        @pl.when(v < NCH)
        def _():
            for h in range(1, W):
                a_copy(h).wait_send()

        for h in range(1, W):
            ov_copy(h).wait_send()
            f_copy(h).wait_send()
        c_ov.wait()
        c_f.wait()

    DMA = pltpu.SemaphoreType.DMA
    V = pltpu.VMEM
    any_spec = pl.BlockSpec(memory_space=pl.ANY)
    return pl.pallas_call(
        kernel,
        name="dress",
        out_shape=(jax.ShapeDtypeStruct((Q, N, RV), F32),
                   jax.ShapeDtypeStruct((R, Q * W, PIECE), F32),
                   jax.ShapeDtypeStruct((R, A), F32)),
        in_specs=[pl.BlockSpec(memory_space=pltpu.HBM)] * 3,
        out_specs=(any_spec,) * 3,
        scratch_shapes=[
            V((CORES, NZ, GRAN, GR, MAIN), F32),
            V((CORES, NZ, HEAD, GR, LANES), F32),
            V((NCH, CORES, NZ, NJ * CH, GR, LANES), F32),
            V((Q, N, RV), F32),
            V((Q, R, N), F32),
            V((R, A), F32),
            V((KP, NP), F32),
            V((ROWS, N), F32),
            V((2 * KP, N), BF16),
            V((A, 2 * KP), BF16),
            V((2 * KP, 2 * VP), BF16),
            V((2 * KP, 2 * VP), BF16),
            V((W, R, Q, PIECE), F32),
            V((W, R, Q, PIECE), F32),
            V((R, Q * W, PIECE), F32),
            V((W, NJ, GR, A), F32),
            V((R, A), F32),
            DMA((NZ, 2)), DMA((NZ, 2)), DMA((NZ, 2)), DMA((NZ, UNITS)), DMA((UNITS,)),
            DMA((W,)), DMA((NCH,)), DMA((W,)), DMA((W,)), DMA((W,)), DMA((W,)),
            DMA((2,)), DMA((1,)), DMA((1,)), DMA((2,)), pltpu.SemaphoreType.REGULAR((2,)),
        ],
        compiler_params=pltpu.CompilerParams(
            collective_id=0, has_side_effects=True, vmem_limit_bytes=40 * 2**20),
    )


def write_out(*refs):
    n = (len(refs) - 1) // 2
    copies = [pltpu.make_async_copy(refs[i], refs[n + i], refs[-1].at[i]) for i in range(n)]
    for c in copies:
        c.start()
    for c in copies:
        c.wait()


def store(arrays):
    return pl.pallas_call(
        write_out,
        name="store",
        out_shape=tuple(jax.ShapeDtypeStruct(a.shape, a.dtype) for a in arrays),
        in_specs=[pl.BlockSpec(memory_space=pl.ANY)] * len(arrays),
        out_specs=(pl.BlockSpec(memory_space=pltpu.HBM),) * len(arrays),
        scratch_shapes=[pltpu.SemaphoreType.DMA((len(arrays),))],
        compiler_params=pltpu.CompilerParams(vmem_limit_bytes=2**20),
    )(*arrays)


def solution(mesh):
    W, D = mesh.shape["vec"], mesh.shape["orb"]

    def shards(chol_occ, chol_vir, singles):
        Q, R, N = chol_occ.shape
        call = make_kernel(W, D, Q, R, chol_vir.shape[1], N, singles.shape[1])
        args = (chol_occ, jnp.swapaxes(chol_vir, 1, 2), singles)
        vir, ov, fock = store(call(*(pltpu.with_memory_space_constraint(a, pltpu.HBM) for a in args)))
        return jnp.swapaxes(vir, 1, 2), jnp.swapaxes(ov, 0, 1), fock

    return jax.shard_map(
        shards,
        mesh=mesh,
        in_specs=(P("vec", "orb", None), P("vec", "orb", None), P("orb", None)),
        out_specs=(P("vec", "orb", None), P(None, "orb", "vec"), P("orb", None)),
        check_vma=False,
    )
```

```python
import jax
import jax.numpy as jnp
from jax import lax
from jax.experimental import pallas as pl
from jax.experimental.pallas import tpu as pltpu
from jax.sharding import PartitionSpec as P

MESH = pl.DeviceIdType.MESH
F32, BF16 = jnp.float32, jnp.bfloat16
LANES = 128
CORES = 2
SKEW = 1
AHEAD = 5
FIRST = 5
RATE = 2


def split(x):
    hi = x.astype(BF16)
    return hi, (x - hi.astype(F32)).astype(BF16)


def dot(a, b):
    return jnp.dot(a, b, preferred_element_type=F32)


def make_kernel(W, D, Q, R, RV, N, A):
    OCC = N - A
    NZ = D // CORES
    GR = 8 if R % 8 == 0 else (4 if R % 4 == 0 else R)
    NJ = R // GR
    ROWS = Q * R
    GRAN = Q * NJ
    MAIN = N // LANES * LANES
    TAIL = N - MAIN
    SLOTS = LANES // TAIL if TAIL else 1
    GROUPS = -(-Q // SLOTS)
    PIECE = A // W
    KP = -(-OCC // LANES) * LANES
    UNITS = Q + 1
    NP = -(-N // LANES) * LANES
    AP = -(-A // LANES) * LANES
    VP = -(-RV // LANES) * LANES
    TILES = AP // LANES
    CH = -(-TILES // W)
    NCH = -(-TILES // CH)
    HT = GROUPS * NJ
    HS = HT + 1
    HEAD = HS + NJ * CH
    LAG = SKEW * max(NZ - 2, 0)
    STEPS = UNITS + LAG
    START = max(FIRST, LAG + 1)
    GATHER = max(START, STEPS - 4)

    def kernel(occ, vir, sing, vloc, ovout, fout,
               gath, head, amps, oloc, sloc, xbuf, drows, tmat, tright, sleft, lwts,
               ovsend, ovrecv, fbuf,
               s_right, s_left, s_part, r_dir, r_part, a_s, a_r, ov_s, ov_r, f_s, f_r,
               in_sem, v_in, ready):
        v = lax.axis_index("vec")
        o = lax.axis_index("orb")
        z = o // CORES
        k = o % CORES
        has_r = z < NZ - 1
        has_l = z > 0
        right = lax.rem(o + CORES, D)
        left = lax.rem(o - CORES + D, D)
        part = z * CORES + (1 - k)

        c_occ = pltpu.make_async_copy(occ, oloc, in_sem.at[0])
        c_sing = pltpu.make_async_copy(sing, sloc, in_sem.at[1])
        c_occ.start()
        c_sing.start()

        c_vir = pltpu.make_async_copy(vir, vloc, v_in.at[0])

        bar = pltpu.get_barrier_semaphore()

        @pl.when(has_r)
        def _():
            pl.semaphore_signal(bar, inc=1, device_id=(v, right), device_id_type=MESH)

        pl.semaphore_signal(bar, inc=1, device_id=(v, part), device_id_type=MESH)
        for h in range(1, W):
            @pl.when(v + h < W)
            def _():
                pl.semaphore_signal(bar, inc=1, device_id=(lax.rem(v + h, W), o), device_id_type=MESH)

        pl.semaphore_wait(bar, has_l.astype(jnp.int32) + v + 1)

        @pl.when(has_l)
        def _():
            pl.semaphore_signal(ready.at[0], inc=1, device_id=(v, left), device_id_type=MESH)

        for h in range(1, W):
            @pl.when(v - h >= 0)
            def _():
                pl.semaphore_signal(ready.at[1], inc=1, device_id=(lax.rem(v - h + W, W), o),
                                    device_id_type=MESH)

        def piece(c, s, u):
            if isinstance(u, str):
                return head.at[c, s], 0, 0
            return gath.at[c, s, pl.ds(u * NJ, NJ)], u + 1, 1

        def remote(s, u, sems, target):
            ref, i, kind = piece(k, s, u)
            return pltpu.make_async_remote_copy(
                src_ref=ref, dst_ref=ref, send_sem=sems.at[kind], recv_sem=r_dir.at[s, i],
                device_id=(v, target), device_id_type=MESH)

        def across(s, u):
            ref, i, kind = piece(k, s, u)
            return pltpu.make_async_remote_copy(
                src_ref=ref, dst_ref=ref, send_sem=s_part.at[kind], recv_sem=r_part.at[i],
                device_id=(v, part), device_id_type=MESH)

        def send_left(u):
            @pl.when(has_l)
            def _():
                remote(z, u, s_left, left).start()

            across(z, u).start()

        def send_right(u):
            @pl.when(has_r)
            def _():
                remote(z, u, s_right, right).start()

        def send_own(u):
            send_left(u)
            send_right(u)

        def relay(h, u):
            @pl.when(z - h >= 0)
            def _():
                s = z - h
                remote(s, u, s_right, right).wait_recv()

                @pl.when(has_r)
                def _():
                    remote(s, u, s_right, right).start()

                across(s, u).start()

            @pl.when(z + h < NZ)
            def _():
                s = z + h
                remote(s, u, s_left, left).wait_recv()

                @pl.when(has_l)
                def _():
                    remote(s, u, s_left, left).start()

                across(s, u).start()

        def from_partner(u):
            if isinstance(u, str):
                ref, i = head.at[1 - k], 0
            else:
                ref, i = gath.at[1 - k, :, pl.ds(u * NJ, NJ)], u + 1
            pltpu.make_async_remote_copy(
                src_ref=ref, dst_ref=ref, send_sem=s_part.at[0], recv_sem=r_part.at[i],
                device_id=(v, part), device_id_type=MESH).wait_recv()

        def finish():
            for kind, ref in enumerate((head, gath)):
                def drain(lo, hi, sems, target):
                    sent = ref.at[k, lo:hi]
                    pltpu.make_async_remote_copy(
                        src_ref=sent, dst_ref=sent, send_sem=sems.at[kind], recv_sem=r_dir.at[0, 0],
                        device_id=(v, target), device_id_type=MESH).wait_send()

                drain(0, NZ, s_part, part)
                for i in range(NZ):
                    @pl.when(z == i)
                    def _():
                        if i < NZ - 1:
                            drain(0, i + 1, s_right, right)
                        if i > 0:
                            drain(i, NZ, s_left, left)

        def a_copy(h):
            w = lax.rem(v + h, W)
            c = lax.rem(v, NCH)
            return pltpu.make_async_remote_copy(
                src_ref=head.at[:, :, pl.ds(HS, NJ * CH)], dst_ref=amps.at[c], send_sem=a_s.at[h],
                recv_sem=a_r.at[c], device_id=(w, o), device_id_type=MESH)

        def a_wait(c):
            @pl.when(c != v)
            def _():
                pltpu.make_async_remote_copy(
                    src_ref=amps.at[c], dst_ref=amps.at[c], send_sem=a_s.at[0],
                    recv_sem=a_r.at[c], device_id=(lax.rem(v + 1, W), o), device_id_type=MESH).wait_recv()

        def repack(q):
            for j in range(NJ):
                gath[k, z, q * NJ + j] = oloc[q, j * GR:(j + 1) * GR, 0:MAIN]

        units = ["h"] + list(range(Q))
        c_occ.wait()
        repack(0)
        send_left(0)
        c_sing.wait()
        full = sloc[...]
        if NCH * CH * LANES > A:
            full = jnp.concatenate([full, jnp.zeros((R, NCH * CH * LANES - A), F32)], axis=1)
        mine = lax.rem(v, NCH)
        for t in range(CH):
            val = full[:, t * LANES:(t + 1) * LANES]
            for c in range(1, NCH):
                at = (c * CH + t) * LANES
                val = jnp.where(mine == c, full[:, at:at + LANES], val)
            for j in range(NJ):
                head[k, z, HS + j * CH + t] = val[j * GR:(j + 1) * GR]
        if TAIL:
            for g in range(GROUPS):
                parts = [oloc[min(g * SLOTS + t, Q - 1), :, MAIN:N] for t in range(SLOTS)]
                packed = jnp.concatenate(parts, axis=1) if SLOTS > 1 else parts[0]
                for j in range(NJ):
                    head[k, z, g * NJ + j, :, 0:SLOTS * TAIL] = packed[j * GR:(j + 1) * GR]
        ri = lax.broadcasted_iota(jnp.int32, (R, KP), 0) + o * R
        ci = lax.broadcasted_iota(jnp.int32, (R, KP), 1)
        mask = ri == ci
        lane = lax.broadcasted_iota(jnp.int32, (GR, LANES), 1)
        tr = jnp.zeros((GR, LANES), F32)
        for q in range(Q):
            dq = jnp.sum(jnp.where(mask, oloc[q, :, 0:KP], 0.0), axis=0, keepdims=True)
            tq = jnp.sum(dq, axis=1, keepdims=True)
            tr = tr + jnp.where(lane == q, jnp.broadcast_to(tq, (GR, LANES)), 0.0)
        head[k, z, HT] = tr
        for q in range(1, Q):
            repack(q)

        for u in units[:AHEAD]:
            if u != 0:
                send_left(u)

        @pl.when(has_r)
        def _():
            pl.semaphore_wait(ready.at[0], 1)

        for u in units[:AHEAD]:
            send_right(u)
        c_vir.start()

        for q in range(Q):
            for r in range(R):
                drows[r * Q + q:r * Q + q + 1, :] = oloc[q, r:r + 1, :]

        for t in range(START):
            if AHEAD <= t + AHEAD < UNITS:
                send_own(units[t + AHEAD])
            for h in range(1, NZ):
                n = t - SKEW * (h - 1)
                if 0 <= n < UNITS:
                    relay(h, units[n])
            if t == LAG:
                from_partner("h")

                @pl.when(v < W - 1)
                def _():
                    pl.semaphore_wait(ready.at[1], W - 1 - v)

                @pl.when(v < NCH)
                def _():
                    for h in range(1, W):
                        a_copy(h).start()

        for c in range(NCH):
            a_wait(c)

            @pl.when(c == v)
            def _():
                amps[c] = head[:, :, HS:HS + NJ * CH]

        xbuf[...] = jnp.zeros_like(xbuf)
        for d in range(D):
            for j in range(NJ):
                at = d * R + j * GR
                for t in range(TILES):
                    xbuf[at:at + GR, t * LANES:(t + 1) * LANES] = (
                        amps[t // CH, d % CORES, d // CORES, j * CH + t % CH])
        amp = xbuf[0:OCC, 0:A]
        tmat[...] = jnp.zeros_like(tmat)
        shifted = jnp.concatenate([jnp.zeros((OCC, OCC), F32), amp], axis=1)
        thi, tlo = split(shifted)
        tmat[0:OCC, :] = thi
        tmat[KP:KP + OCC, :] = tlo
        thi, tlo = split(jnp.transpose(xbuf[:, 0:AP])[0:A])
        tright[:, 0:KP] = thi
        tright[:, KP:2 * KP] = tlo
        ahi, alo = split(xbuf[:, 0:A])
        pick = (lax.broadcasted_iota(jnp.int32, (A, VP), 0)
                == lax.broadcasted_iota(jnp.int32, (A, VP), 1) + o * RV)
        pick = jnp.where(pick, 1.0, 0.0).astype(BF16)
        shi = dot(ahi, pick).astype(BF16)
        sleft[0:KP, 0:VP] = shi
        sleft[KP:2 * KP, 0:VP] = shi
        sleft[0:KP, VP:2 * VP] = dot(alo, pick).astype(BF16)
        sleft[KP:2 * KP, VP:2 * VP] = jnp.zeros((KP, VP), BF16)
        lwts[...] = jnp.zeros_like(lwts)

        keep = lax.broadcasted_iota(jnp.int32, (ROWS, KP), 1) < OCC
        hi, lo = split(jnp.where(keep, drows[:, 0:KP], 0.0))
        extra = dot(jnp.concatenate([hi, hi], axis=1), tmat[...]) + dot(lo, tmat[0:KP, :])
        drows[...] = drows[...] + extra
        for w in range(W):
            sl = drows[:, OCC + w * PIECE:OCC + (w + 1) * PIECE]
            for r in range(R):
                ovsend[w, r] = sl[r * Q:(r + 1) * Q]
        total = head[0, 0, HT]
        for d in range(1, D):
            total = total + head[d % CORES, d // CORES, HT]
        rid = lax.broadcasted_iota(jnp.int32, (R, ROWS), 0) * Q
        cid = lax.broadcasted_iota(jnp.int32, (R, ROWS), 1)
        wts = jnp.zeros((R, ROWS), F32)
        for q in range(Q):
            wts = wts + jnp.where(cid == rid + q, jnp.broadcast_to(total[0:1, q:q + 1], (R, ROWS)), 0.0)
        whi, wlo = split(wts)
        dhi, dlo = split(drows[...])
        fock = (dot(whi, dhi) + (dot(whi, dlo) + dot(wlo, dhi)))[:, OCC:]
        for j in range(NJ):
            fbuf[v, j] = fock[j * GR:(j + 1) * GR]

        def ov_copy(h):
            w = lax.rem(v + h, W)
            return pltpu.make_async_remote_copy(
                src_ref=ovsend.at[w], dst_ref=ovrecv.at[v], send_sem=ov_s.at[h],
                recv_sem=ov_r.at[h], device_id=(w, o), device_id_type=MESH)

        def f_copy(h):
            w = lax.rem(v + h, W)
            return pltpu.make_async_remote_copy(
                src_ref=fbuf.at[v], dst_ref=fbuf.at[v], send_sem=f_s.at[h],
                recv_sem=f_r.at[h], device_id=(w, o), device_id_type=MESH)

        for h in range(1, W):
            ov_copy(h).start()
            f_copy(h).start()
        ovrecv[v] = ovsend[v]

        c_vir.wait()

        def dress(q):
            from_partner(q)
            if TAIL:
                shift = lax.rem(LANES - lax.rem(q, SLOTS) * TAIL, LANES)
            for d in range(D):
                for j in range(NJ):
                    at = d * R + j * GR
                    xbuf[at:at + GR, 0:MAIN] = gath[d % CORES, d // CORES, q * NJ + j]
                    if TAIL:
                        t = pltpu.roll(head[d % CORES, d // CORES, (q // SLOTS) * NJ + j], shift, axis=1)
                        xbuf[at:at + GR, MAIN:N] = t[:, 0:TAIL]
            hi, lo = split(jnp.transpose(xbuf[...])[0:N])
            prod = dot(jnp.concatenate([hi, lo], axis=1), sleft[...])
            prod = prod[:, 0:VP] + prod[:, VP:2 * VP]
            vloc[q] = vloc[q] - prod[:, 0:RV]
            hi, lo = split(vloc[q, 0:OCC, :])
            lwts[0:OCC, 0:RV] = hi
            lwts[KP:KP + OCC, 0:RV] = hi
            lwts[0:OCC, VP:VP + RV] = lo
            prod = dot(tright[...], lwts[...])
            prod = prod[:, 0:VP] + prod[:, VP:2 * VP]
            vloc[q, OCC:N, :] = vloc[q, OCC:N, :] + prod[:, 0:RV]

        def collect():
            for h in range(1, W):
                ov_copy(h).wait_recv()
                f_copy(h).wait_recv()
            for w in range(W):
                for r in range(R):
                    ovout[r, w * Q:(w + 1) * Q, :] = ovrecv[w, r]
            for j in range(NJ):
                acc = fbuf[0, j]
                for w in range(1, W):
                    acc = acc + fbuf[w, j]
                fout[j * GR:(j + 1) * GR, :] = acc / (Q * W)

        def done(t):
            return jnp.where(t == STEPS - 1, Q, jnp.minimum(t - LAG - 1, RATE * (t - START + 1)))

        @pl.loop(START, STEPS)
        def _(t):
            @pl.when(t + AHEAD < UNITS)
            def _():
                send_own(t + AHEAD - 1)

            for h in range(1, NZ):
                n = t - SKEW * (h - 1)

                @pl.when(n < UNITS)
                def _():
                    relay(h, n - 1)

            lo = jnp.where(t == START, 0, done(t - 1))

            @pl.loop(lo, done(t))
            def _(q):
                dress(q)

            @pl.when(t == GATHER)
            def _():
                collect()

        finish()

        @pl.when(v < NCH)
        def _():
            for h in range(1, W):
                a_copy(h).wait_send()

        for h in range(1, W):
            ov_copy(h).wait_send()
            f_copy(h).wait_send()

    DMA = pltpu.SemaphoreType.DMA
    V = pltpu.VMEM
    return pl.pallas_call(
        kernel,
        name="dress",
        out_shape=(jax.ShapeDtypeStruct((Q, N, RV), F32),
                   jax.ShapeDtypeStruct((R, Q * W, PIECE), F32),
                   jax.ShapeDtypeStruct((R, A), F32)),
        in_specs=[pl.BlockSpec(memory_space=pltpu.HBM)] * 3,
        out_specs=(pl.BlockSpec(memory_space=pltpu.VMEM),) * 3,
        scratch_shapes=[
            V((CORES, NZ, GRAN, GR, MAIN), F32),
            V((CORES, NZ, HEAD, GR, LANES), F32),
            V((NCH, CORES, NZ, NJ * CH, GR, LANES), F32),
            V((Q, R, N), F32),
            V((R, A), F32),
            V((KP, NP), F32),
            V((ROWS, N), F32),
            V((2 * KP, N), BF16),
            V((A, 2 * KP), BF16),
            V((2 * KP, 2 * VP), BF16),
            V((2 * KP, 2 * VP), BF16),
            V((W, R, Q, PIECE), F32),
            V((W, R, Q, PIECE), F32),
            V((W, NJ, GR, A), F32),
            DMA((2,)), DMA((2,)), DMA((2,)), DMA((NZ, UNITS)), DMA((UNITS,)),
            DMA((W,)), DMA((NCH,)), DMA((W,)), DMA((W,)), DMA((W,)), DMA((W,)),
            DMA((2,)), DMA((1,)), pltpu.SemaphoreType.REGULAR((2,)),
        ],
        compiler_params=pltpu.CompilerParams(
            collective_id=0, has_side_effects=True, vmem_limit_bytes=40 * 2**20),
    )


def write_out(*refs):
    n = (len(refs) - 1) // 2
    copies = [pltpu.make_async_copy(refs[i], refs[n + i], refs[-1].at[i]) for i in range(n)]
    for c in copies:
        c.start()
    for c in copies:
        c.wait()


def store(arrays):
    return pl.pallas_call(
        write_out,
        name="store",
        out_shape=tuple(jax.ShapeDtypeStruct(a.shape, a.dtype) for a in arrays),
        in_specs=[pl.BlockSpec(memory_space=pl.ANY)] * len(arrays),
        out_specs=(pl.BlockSpec(memory_space=pltpu.HBM),) * len(arrays),
        scratch_shapes=[pltpu.SemaphoreType.DMA((len(arrays),))],
        compiler_params=pltpu.CompilerParams(vmem_limit_bytes=2**20),
    )(*arrays)


def solution(mesh):
    W, D = mesh.shape["vec"], mesh.shape["orb"]

    def shards(chol_occ, chol_vir, singles):
        Q, R, N = chol_occ.shape
        call = make_kernel(W, D, Q, R, chol_vir.shape[1], N, singles.shape[1])
        args = (chol_occ, jnp.swapaxes(chol_vir, 1, 2), singles)
        vir, ov, fock = store(call(*(pltpu.with_memory_space_constraint(a, pltpu.HBM) for a in args)))
        return jnp.swapaxes(vir, 1, 2), jnp.swapaxes(ov, 0, 1), fock

    return jax.shard_map(
        shards,
        mesh=mesh,
        in_specs=(P("vec", "orb", None), P("vec", "orb", None), P("orb", None)),
        out_specs=(P("vec", "orb", None), P(None, "orb", "vec"), P("orb", None)),
        check_vma=False,
    )
```
